32 devices in a mesh: depth: 16 (over z, x, core), freq: 2 (over y).
Axes of the slice: x: 2, y: 2, z: 4, core: 2. Of those that a mesh axis runs over, the one named last changes fastest.
Arguments:
- propagator: bfloat16 [16, 4, 2, 1024, 1024], P('depth', 'freq'), may hold values from -0.125 to 0.125
- incident: bfloat16 [16, 4, 1024, 256], P('depth', 'freq'), may hold values from -6 to 6
- coeffs: float32 [16, 1024, 64], P('depth'), may hold values from -4 to 4
Outputs:
- upgoing: bfloat16 [16, 4, 1024, 256], P('depth', 'freq')
- gradient: float32 [16, 1024, 64], P('depth', 'freq')
- reflected: bfloat16 [16, 4, 1024, 256], P('depth', 'freq')
The draws below stay inside these ranges and needn't reach their ends.
All inputs are finite; a program needn't handle non-finite values.
Results may differ from the reference program's by a relative error of at most 0.024.
Values may be sent and summed in bfloat16 or wider, within the bound.
A program may use at most 64 MiB of HBM per device.

```python
import jax
import jax.numpy as jnp
from jax import lax

NX = 1024
NA = 64
SHOTS = 128
ITERS = 3
LEVELS = 16
FREQS = 4


def block_scale(key, extent, cuts, low, top_value):
    def one(position, parts):
        draws = jax.random.uniform(jax.random.fold_in(jax.random.fold_in(key, 6), position), (parts,), jnp.float32, low / len(cuts), top_value / len(cuts))
        return jnp.repeat(jnp.exp(draws), extent[position] // parts).reshape((-1,) + (1,) * (len(extent) - position - 1))

    gain = one(*cuts[0])
    for cut in cuts[1:]:
        gain = gain * one(*cut)
    return gain


def scatter_about(rng, extent, width, limit, pieces=(), kind=jnp.bfloat16):
    drawn = width * jax.random.normal(rng, extent, jnp.float32)
    if pieces:
        drawn = drawn * block_scale(rng, extent, pieces, -0.22, 0.18)
    return jnp.clip(drawn, -limit, limit).astype(kind)


def setup_inputs(seed: int = 0) -> dict:
    streams_of = jax.random.split(jax.random.key(seed), 4)
    propagator = scatter_about(streams_of[0], (LEVELS, FREQS, 2, NX, NX), (2 * NX) ** -0.5, 0.125, ((0, 16), (1, 2)))
    incident = scatter_about(streams_of[1], (LEVELS, FREQS, NX, 2 * SHOTS), 1.0, 6.0, ((0, 16), (1, 2)))
    coeffs = scatter_about(streams_of[2], (LEVELS, NX, NA), 1.0, 4.0, ((0, 16),), jnp.float32)
    return {"propagator": propagator, "incident": incident, "coeffs": coeffs}


def angle_table():
    angle = jnp.arange(NA, dtype=jnp.float32)[:, None] + 0.5
    place = jnp.arange(NX, dtype=jnp.float32)[None, :] + 0.5
    return (jnp.sqrt(2.0 / NX) * jnp.cos(jnp.pi * angle * place / NX)).astype(jnp.bfloat16)

def angles_of(table, field):
    return jnp.einsum('ay,lfys->lfas', table.astype(jnp.float32), field.astype(jnp.float32)).astype(jnp.bfloat16)

def reflect(kernel, table, field):
    return jnp.einsum('lxa,lfas->lfxs', kernel.astype(jnp.float32), angles_of(table, field).astype(jnp.float32))

def apply_level(weights, field, transpose):
    wf = weights.astype(jnp.float32)
    ff = field.astype(jnp.float32)
    form = 'fyx,fys->fxs' if transpose else 'fxy,fys->fxs'
    first = jnp.einsum(form, wf[:, 0], ff)
    second = jnp.einsum(form, wf[:, 1], ff)
    return first + jnp.concatenate([-second[..., SHOTS:], second[..., :SHOTS]], -1)

def propagate(propagator, field, transpose):
    return lax.map(lambda pair: apply_level(pair[0], pair[1], transpose), (propagator, field))

def reference(propagator, incident, coeffs):
    table = angle_table()
    kernel = (coeffs * table.T.astype(jnp.float32)[None]).astype(jnp.bfloat16)
    down = jnp.zeros(incident.shape, jnp.bfloat16)
    upgoing = jnp.zeros(incident.shape, jnp.bfloat16)
    for step in range(ITERS):
        send_down = (down.astype(jnp.float32) - reflect(kernel, table, upgoing)).astype(jnp.bfloat16)
        total = (incident.astype(jnp.float32) + down.astype(jnp.float32)).astype(jnp.bfloat16)
        send_up = (upgoing.astype(jnp.float32) + reflect(kernel, table, total)).astype(jnp.bfloat16)
        blank = jnp.zeros_like(send_down[:1])
        above = jnp.concatenate([blank, send_down[:-1]], 0)
        below = jnp.concatenate([send_up[1:], blank], 0)
        down = propagate(propagator, above, False).astype(jnp.bfloat16)
        upgoing = propagate(propagator, below, True).astype(jnp.bfloat16)
    total = (incident.astype(jnp.float32) + down.astype(jnp.float32)).astype(jnp.bfloat16)
    final_angles = angles_of(table, total)
    summed = jnp.einsum('lfxs,lfas->lxa', upgoing.astype(jnp.float32), final_angles.astype(jnp.float32))
    gradient = summed / jnp.sqrt(jnp.float32(SHOTS * FREQS))
    updated = coeffs - gradient
    new_kernel = (updated * table.T.astype(jnp.float32)[None]).astype(jnp.bfloat16)
    reflected = jnp.einsum('lxa,lfas->lfxs', new_kernel.astype(jnp.float32), final_angles.astype(jnp.float32)).astype(jnp.bfloat16)
    return (upgoing, gradient, reflected)
```

```python
import jax
import jax.numpy as jnp
from jax import lax
from jax.sharding import PartitionSpec as P

BF = jnp.bfloat16
F32 = jnp.float32


def passed_along(block, axis, distance):
    devices = range(lax.axis_size(axis))
    route = [(i - distance, i) for i in devices if i - distance in devices]
    return lax.ppermute(block, axis, route)


def angle_table(count, points):
    angle = jnp.arange(count, dtype=F32)[:, None] + 0.5
    place = jnp.arange(points, dtype=F32)[None, :] + 0.5
    return (jnp.sqrt(2.0 / points) * jnp.cos(jnp.pi * angle * place / points)).astype(BF)


def dot(a, b):
    return jnp.dot(a, b, preferred_element_type=F32)


def dot_nt(a, b):
    return lax.dot_general(a, b, (((1,), (1,)), ((), ())), preferred_element_type=F32)


def dot_tn(a, b):
    return lax.dot_general(a, b, (((0,), (0,)), ((), ())), preferred_element_type=F32)


def turned(field):
    half = field.shape[-1] // 2
    return jnp.concatenate([-field[:, half:], field[:, :half]], 1)


def paired(field):
    return jnp.concatenate([field, turned(field)], 0)


def complex_rows(rows, real, imag):
    half = rows.shape[0] // 2
    first = dot(rows, real)
    second = dot(rows, imag)
    return (
        (first[:half] - second[half:]).astype(BF),
        (first[half:] + second[:half]).astype(BF),
    )


def small(table, real, imag):
    return jnp.concatenate([dot_nt(table, real), dot_nt(table, imag)], 1).astype(BF)


def local(propagator, incident, coeffs):
    weights = propagator[0]
    source = incident[0]
    count = coeffs.shape[2]
    points = incident.shape[2]
    width = incident.shape[3]
    nfreq = source.shape[0]
    table = angle_table(count, points)
    kernel = (coeffs[0].T * table.astype(F32)).astype(BF)
    kernel_up = passed_along(kernel, "depth", -1)
    kernel_down = passed_along(kernel, "depth", 1)
    outs = []
    finals = []
    partial_value = 0.0
    for f in range(nfreq):
        real, imag = weights[f, 0], weights[f, 1]
        a0 = dot(table, source[f]).astype(BF)
        a1 = passed_along(a0, "depth", -1)
        a2 = passed_along(a1, "depth", -1)
        a3 = passed_along(a2, "depth", -1)
        lhs = jnp.concatenate([kernel_up, table], 0)
        one = jnp.concatenate([dot(lhs, real), dot(lhs, imag)], 0).astype(BF)
        g1r, g1i = one[:count], one[2 * count : 3 * count]
        one_up = passed_along(one, "depth", -1)
        s1r_up, s1i_up = one_up[count : 2 * count], one_up[3 * count :]
        two_r, two_i = complex_rows(one_up, real, imag)
        g2r, s2r = two_r[:count], two_r[count:]
        g2i, s2i = two_i[:count], two_i[count:]
        g2_up = passed_along(jnp.concatenate([g2r, g2i], 0), "depth", -1)
        g3r, g3i = complex_rows(g2_up, real, imag)
        tg1 = small(table, g1r, g1i)
        tg2 = small(table, g2r, g2i)
        b0 = dot(tg1, paired(a1)).astype(BF)
        b_down = passed_along(b0, "depth", 1)
        c0 = (dot(tg2, paired(a2)) + dot(tg1, paired(a1))).astype(BF)
        th1 = jnp.concatenate([dot_nt(s1r_up, kernel), dot_nt(s1i_up, kernel)], 1).astype(BF)
        th2 = jnp.concatenate([dot_nt(s2r, kernel_down), dot_nt(s2i, kernel_down)], 1).astype(BF)
        d1 = (a1.astype(F32) - dot(th1, paired(b0))).astype(BF)
        e1 = (dot(th2, paired(b_down)) + dot(th1, paired(c0))).astype(BF)
        e0 = passed_along(e1, "depth", 1)
        final = (a0.astype(F32) - e0.astype(F32)).astype(BF)
        up = dot_tn(
            jnp.concatenate([g3r, g3i, g2r, g2i, g1r, g1i], 0),
            jnp.concatenate([paired(a3), paired(a2), paired(d1)], 0),
        ).astype(BF)
        outs.append(up)
        finals.append(final)
        partial_value = partial_value + dot_nt(up, final)
    upgoing = jnp.stack(outs)
    scale = 1.0 / jnp.sqrt(F32(width // 2 * nfreq * lax.axis_size("freq")))
    partial_value = partial_value * scale
    rows = points // lax.axis_size("freq")
    start = lax.axis_index("freq") * rows
    grad_rows = lax.psum_scatter(
        partial_value.astype(BF), "freq", scatter_dimension=0, tiled=True
    ).astype(F32)
    mine = lax.dynamic_slice_in_dim(coeffs[0], start, rows, 0) - grad_rows
    updated = lax.all_gather(mine.astype(BF), "freq", axis=0, tiled=True).astype(mine.dtype)
    new_kernel = (updated * table.T.astype(F32)).astype(BF)
    reflected = jnp.stack([dot(new_kernel, final).astype(BF) for final in finals])
    return (upgoing[None], grad_rows[None], reflected[None])


def solution(mesh):
    return jax.shard_map(
        local,
        mesh=mesh,
        in_specs=(
            P("depth", "freq", None, None, None),
            P("depth", "freq", None, None),
            P("depth", None, None),
        ),
        out_specs=(
            P("depth", "freq", None, None),
            P("depth", "freq", None),
            P("depth", "freq", None, None),
        ),
        check_vma=False,
    )
```

```python
import functools

import jax
import jax.numpy as jnp
from jax import lax
from jax.experimental import pallas as pl
from jax.experimental.pallas import tpu as pltpu
from jax.sharding import PartitionSpec as P

BF = jnp.bfloat16
F32 = jnp.float32
TILE = 256


def dot(a, b):
    return jnp.dot(a, b, preferred_element_type=F32)


def dot_nt(a, b):
    return lax.dot_general(a, b, (((1,), (1,)), ((), ())), preferred_element_type=F32)


def dot_tn(a, b):
    return lax.dot_general(a, b, (((0,), (0,)), ((), ())), preferred_element_type=F32)


def turned(field):
    half = field.shape[-1] // 2
    return jnp.concatenate([-field[:, half:], field[:, :half]], 1)


def angle_table(count, points):
    angle = lax.broadcasted_iota(jnp.int32, (count, points), 0).astype(F32) + 0.5
    place = lax.broadcasted_iota(jnp.int32, (count, points), 1).astype(F32) + 0.5
    return ((2.0 / points) ** 0.5 * jnp.cos(jnp.pi * angle * place / points)).astype(BF)


def body(
    nd, nf, prop, inc, coef, up_out, grad_out, refl_out,
    w, src, cf, table, k0, k_up, k_dn, a, q, s1, s1_in, s2, g, g1_in, g2_in,
    b0, b_in, e1, e_in, fin, up_v, part_s, part_in, grad_t, grad_v, refl_v,
    in_sem, out_sem, send, recv, fsend, frecv,
):
    me = lax.axis_index("depth")
    fme = lax.axis_index("freq")
    nfreq, _, points, _ = w.shape
    count = table.shape[0]
    half = src.shape[2] // 2
    has_above = me > 0
    has_below = me < nd - 1
    above = lax.rem(me + nd - 1, nd)
    below = lax.rem(me + 1, nd)

    coef_in = pltpu.make_async_copy(coef.at[0], cf, in_sem.at[0])
    src_in = pltpu.make_async_copy(inc.at[0], src, in_sem.at[1])
    w_in = [
        [
            pltpu.make_async_copy(prop.at[0, f, p], w.at[f, p], in_sem.at[2 + 2 * f + p])
            for p in range(2)
        ]
        for f in range(nfreq)
    ]
    coef_in.start()
    for f in range(nfreq):
        w_in[f][0].start()
        w_in[f][1].start()
        if f == 0:
            src_in.start()

    barrier = pltpu.get_barrier_semaphore()

    @pl.when(has_above)
    def _():
        pl.semaphore_signal(barrier, 1, device_id={"depth": above})

    @pl.when(has_below)
    def _():
        pl.semaphore_signal(barrier, 1, device_id={"depth": below})

    for d in range(1, nf):
        pl.semaphore_signal(barrier, 1, device_id={"freq": lax.rem(fme + d, nf)})

    def ahead(x, y, i):
        return pltpu.make_async_remote_copy(
            x, y, send.at[i], recv.at[i], device_id={"depth": above}
        )

    def behind(x, y, i):
        return pltpu.make_async_remote_copy(
            x, y, send.at[i], recv.at[i], device_id={"depth": below}
        )

    c_kup = ahead(k0, k_up, 0)
    c_kdn = behind(k0, k_dn, 1)
    c_a = [ahead(a.at[j], a.at[j + 1], 2 + j) for j in range(3)]
    c_b = behind(b0, b_in, 5)
    c_e = behind(e1, e_in, 6)
    c_s1 = [ahead(s1.at[f], s1_in.at[f], 7 + f) for f in range(nfreq)]
    c_g1 = [
        ahead(g.at[f, pl.ds(4 * count, 2 * count)], g1_in.at[f], 7 + nfreq + f)
        for f in range(nfreq)
    ]
    c_g2 = [
        ahead(g.at[f, pl.ds(2 * count, 2 * count)], g2_in.at[f], 7 + 2 * nfreq + f)
        for f in range(nfreq)
    ]
    ups = [c_kup, *c_a, *c_s1, *c_g1, *c_g2]
    downs = [c_kdn, c_b, c_e]

    def start_up(c):
        pl.when(has_above)(c.start)

    def start_down(c):
        pl.when(has_below)(c.start)

    def take(c, there, ref, i=None):
        pl.when(there)(c.wait_recv)

        @pl.when(jnp.logical_not(there))
        def _():
            if i is None:
                ref[...] = jnp.zeros(ref.shape, ref.dtype)
            else:
                ref[i] = jnp.zeros(ref.shape[1:], ref.dtype)

    table[...] = angle_table(count, points)
    coef_in.wait()
    cf_t = cf[...].T
    k0[...] = (cf_t * table[...].astype(F32)).astype(BF)

    inside = jnp.logical_and(has_above, has_below)
    pl.when(inside)(lambda: pl.semaphore_wait(barrier, nf + 1))
    pl.when(jnp.logical_not(inside))(lambda: pl.semaphore_wait(barrier, nf))
    start_up(c_kup)
    start_down(c_kdn)

    def tiles(step):
        def one(c, carry):
            step(pl.ds(pl.multiple_of(c * TILE, TILE), TILE))
            return carry

        lax.fori_loop(0, points // TILE, one, 0)

    def real_times(rows, f, out, base):
        def step(cols):
            for p in range(2):
                out[f, pl.ds(base + p * count, count), cols] = dot(
                    rows[...], w[f, p, :, cols]
                ).astype(BF)

        tiles(step)

    def complex_times(rows, f, out, base):
        def step(cols):
            x = rows[f]
            first = dot(x, w[f, 0, :, cols])
            second = dot(x, w[f, 1, :, cols])
            out[f, pl.ds(base, count), cols] = (first[:count] - second[count:]).astype(BF)
            out[f, pl.ds(base + count, count), cols] = (first[count:] + second[:count]).astype(BF)

        tiles(step)

    for f in range(nfreq):
        w_in[f][0].wait()
        w_in[f][1].wait()
        real_times(table, f, s1, 0)
        start_up(c_s1[f])
    src_in.wait()
    for f in range(nfreq):
        a[0, f] = dot(table[...], src[f]).astype(BF)
    start_up(c_a[0])

    take(c_kup, has_below, k_up)
    for f in range(nfreq):
        real_times(k_up, f, g, 4 * count)
        start_up(c_g1[f])

    def mixed(pair, field):
        n = pair.shape[1] // 2
        return dot(pair[:, :n], field) + dot(pair[:, n:], turned(field))

    take(c_a[0], has_below, a, 1)
    start_up(c_a[1])
    tg1 = []
    for f in range(nfreq):
        tg1.append(dot_nt(table[...], g[f, pl.ds(4 * count, 2 * count)]).astype(BF))
        b0[f] = mixed(tg1[f], a[1, f]).astype(BF)
    start_down(c_b)

    th1 = []
    for f in range(nfreq):
        take(c_s1[f], has_below, s1_in, f)
        complex_times(s1_in, f, s2, 0)
        th1.append(
            [dot_nt(s1_in[f, pl.ds(p * count, count)], k0[...]).astype(BF) for p in range(2)]
        )
        low = dot(th1[f][0], b0[f]) + dot(th1[f][1], turned(b0[f]))
        d1 = (a[1, f].astype(F32) - low).astype(BF)
        q[f, pl.ds(4 * count, count)] = d1
        q[f, pl.ds(5 * count, count)] = turned(d1)
    take(c_a[1], has_below, a, 2)
    start_up(c_a[2])
    take(c_kdn, has_above, k_dn)
    take(c_b, has_above, b_in)

    for f in range(nfreq):
        take(c_g1[f], has_below, g1_in, f)
        complex_times(g1_in, f, g, 2 * count)
        start_up(c_g2[f])

    for f in range(nfreq):
        tg2 = dot_nt(table[...], g[f, pl.ds(2 * count, 2 * count)]).astype(BF)
        c0 = (mixed(tg2, a[2, f]) + mixed(tg1[f], a[1, f])).astype(BF)
        th2 = [dot_nt(s2[f, pl.ds(p * count, count)], k_dn[...]).astype(BF) for p in range(2)]
        e1[f] = (
            dot(th2[0], b_in[f])
            + dot(th2[1], turned(b_in[f]))
            + dot(th1[f][0], c0)
            + dot(th1[f][1], turned(c0))
        ).astype(BF)
    start_down(c_e)
    take(c_a[2], has_below, a, 3)
    for f in range(nfreq):
        q[f, pl.ds(0, count)] = a[3, f]
        q[f, pl.ds(count, count)] = turned(a[3, f])
        q[f, pl.ds(2 * count, count)] = a[2, f]
        q[f, pl.ds(3 * count, count)] = turned(a[2, f])
    take(c_e, has_above, e_in)
    for f in range(nfreq):
        fin[f] = (a[0, f].astype(F32) - e_in[f].astype(F32)).astype(BF)

    up_copies = []
    for f in range(nfreq):
        take(c_g2[f], has_below, g2_in, f)
        complex_times(g2_in, f, g, 0)

        def field(cols):
            value = dot_tn(g[f, :, cols], q[f]).astype(BF)
            up_v[f, cols] = value
            corr = dot_nt(fin[f], value)
            if f == 0:
                grad_t[:, cols] = corr
            else:
                grad_t[:, cols] += corr

        tiles(field)
        up_copies.append(pltpu.make_async_copy(up_v.at[f], up_out.at[0, f], out_sem.at[f]))
        up_copies[f].start()

    scale = 1.0 / (half * nfreq * nf) ** 0.5
    grad_t[...] = grad_t[...] * scale
    part_s[...] = grad_t[...].astype(BF)
    c_f = [
        pltpu.make_async_remote_copy(
            part_s, part_in.at[d - 1], fsend.at[d - 1], frecv.at[d - 1],
            device_id={"freq": lax.rem(fme + d, nf)},
        )
        for d in range(1, nf)
    ]
    for c in c_f:
        c.start()
    for d, c in enumerate(c_f):
        c.wait_recv()
        grad_t[...] += part_in[d].astype(F32)

    rows = points // nf
    k0_new = ((cf_t - grad_t[...]) * table[...].astype(F32)).astype(BF)
    mine = pl.ds(pl.multiple_of(fme * rows, rows), rows)
    refl_copies = []
    pl.when(has_above)(c_kup.wait_send)
    pl.when(has_below)(c_kdn.wait_send)
    k0[...] = k0_new
    for f in range(nfreq):

        def shine(cols):
            refl_v[f, cols] = dot_tn(k0[:, cols], fin[f]).astype(BF)

        tiles(shine)
        refl_copies.append(
            pltpu.make_async_copy(refl_v.at[f], refl_out.at[0, f], out_sem.at[nfreq + f])
        )
        refl_copies[f].start()
    grad_v[...] = grad_t[:, mine].T
    grad_copy = pltpu.make_async_copy(grad_v, grad_out.at[0], out_sem.at[2 * nfreq])
    grad_copy.start()

    for c in ups[1:]:
        pl.when(has_above)(c.wait_send)
    for c in downs[1:]:
        pl.when(has_below)(c.wait_send)
    for c in c_f:
        c.wait_send()
    for c in (*up_copies, *refl_copies, grad_copy):
        c.wait()


def solution(mesh):
    nd, nf = mesh.shape["depth"], mesh.shape["freq"]

    def local(propagator, incident, coeffs):
        _, nfreq, points, width = incident.shape
        count = coeffs.shape[2]
        rows = points // nf
        field = (nfreq, points, width)
        angles = (nfreq, count, width)
        messages = 7 + 3 * nfreq
        hbm = pl.BlockSpec(memory_space=pl.ANY)
        v = pltpu.VMEM
        return pl.pallas_call(
            functools.partial(body, nd, nf),
            out_shape=(
                jax.ShapeDtypeStruct((1, *field), BF),
                jax.ShapeDtypeStruct((1, rows, count), F32),
                jax.ShapeDtypeStruct((1, *field), BF),
            ),
            in_specs=[hbm] * 3,
            out_specs=[hbm] * 3,
            scratch_shapes=[
                v((nfreq, 2, points, points), BF),
                v(field, BF),
                v((points, count), F32),
                v((count, points), BF),
                v((count, points), BF),
                v((count, points), BF),
                v((count, points), BF),
                v((4, *angles), BF),
                v((nfreq, 6 * count, width), BF),
                v((nfreq, 2 * count, points), BF),
                v((nfreq, 2 * count, points), BF),
                v((nfreq, 2 * count, points), BF),
                v((nfreq, 6 * count, points), BF),
                v((nfreq, 2 * count, points), BF),
                v((nfreq, 2 * count, points), BF),
                v(angles, BF),
                v(angles, BF),
                v(angles, BF),
                v(angles, BF),
                v(angles, BF),
                v(field, BF),
                v((count, points), BF),
                v((max(nf - 1, 1), count, points), BF),
                v((count, points), F32),
                v((rows, count), F32),
                v(field, BF),
                pltpu.SemaphoreType.DMA((2 + 2 * nfreq,)),
                pltpu.SemaphoreType.DMA((2 * nfreq + 1,)),
                pltpu.SemaphoreType.DMA((messages,)),
                pltpu.SemaphoreType.DMA((messages,)),
                pltpu.SemaphoreType.DMA((max(nf - 1, 1),)),
                pltpu.SemaphoreType.DMA((max(nf - 1, 1),)),
            ],
            compiler_params=pltpu.CompilerParams(
                collective_id=0, has_side_effects=True, vmem_limit_bytes=60 * 1024 * 1024
            ),
            name="bremmer",
        )(propagator, incident, coeffs)

    return jax.shard_map(
        local,
        mesh=mesh,
        in_specs=(
            P("depth", "freq", None, None, None),
            P("depth", "freq", None, None),
            P("depth", None, None),
        ),
        out_specs=(
            P("depth", "freq", None, None),
            P("depth", "freq", None),
            P("depth", "freq", None, None),
        ),
        check_vma=False,
    )
```

```python
import functools

import jax
import jax.numpy as jnp
from jax import lax
from jax.experimental import pallas as pl
from jax.experimental.pallas import tpu as pltpu
from jax.sharding import PartitionSpec as P

BF = jnp.bfloat16
F32 = jnp.float32
TILE = 256


def dot(a, b):
    return jnp.dot(a, b, preferred_element_type=F32)


def dot_nt(a, b):
    return lax.dot_general(a, b, (((1,), (1,)), ((), ())), preferred_element_type=F32)


def dot_tn(a, b):
    return lax.dot_general(a, b, (((0,), (0,)), ((), ())), preferred_element_type=F32)


def turned(field):
    half = field.shape[-1] // 2
    return jnp.concatenate([-field[:, half:], field[:, :half]], 1)


def angle_table(count, points):
    angle = lax.broadcasted_iota(jnp.int32, (count, points), 0).astype(F32) + 0.5
    place = lax.broadcasted_iota(jnp.int32, (count, points), 1).astype(F32) + 0.5
    return ((2.0 / points) ** 0.5 * jnp.cos(jnp.pi * angle * place / points)).astype(BF)


def body(
    nd, nf, prop, inc, coef, up_out, grad_out, kernel_out, fin_out,
    w, src, cf, table, k0, k_up, k_dn, a, q, s1, s1_in, s2, g, g1_in, g2_in,
    b0, b_in, e1, e_in, fin, up_v, part_s, part_in, grad_t,
    in_sem, out_sem, send, recv, fsend, frecv,
):
    me = lax.axis_index("depth")
    fme = lax.axis_index("freq")
    nfreq, _, points, _ = w.shape
    count = table.shape[0]
    half = src.shape[2] // 2
    has_above = me > 0
    has_below = me < nd - 1
    above = lax.rem(me + nd - 1, nd)
    below = lax.rem(me + 1, nd)

    coef_in = pltpu.make_async_copy(coef.at[0], cf, in_sem.at[0])
    src_in = pltpu.make_async_copy(inc.at[0], src, in_sem.at[1])
    w_in = [
        [
            pltpu.make_async_copy(prop.at[0, f, p], w.at[f, p], in_sem.at[2 + 2 * f + p])
            for p in range(2)
        ]
        for f in range(nfreq)
    ]
    coef_in.start()
    src_in.start()
    for f in range(nfreq):
        w_in[f][0].start()
        w_in[f][1].start()

    barrier = pltpu.get_barrier_semaphore()

    @pl.when(has_above)
    def _():
        pl.semaphore_signal(barrier, 1, device_id={"depth": above})

    @pl.when(has_below)
    def _():
        pl.semaphore_signal(barrier, 1, device_id={"depth": below})

    for d in range(1, nf):
        pl.semaphore_signal(barrier, 1, device_id={"freq": lax.rem(fme + d, nf)})

    def ahead(x, y, i):
        return pltpu.make_async_remote_copy(
            x, y, send.at[i], recv.at[i], device_id={"depth": above}
        )

    def behind(x, y, i):
        return pltpu.make_async_remote_copy(
            x, y, send.at[i], recv.at[i], device_id={"depth": below}
        )

    c_kup = ahead(k0, k_up, 0)
    c_kdn = behind(k0, k_dn, 1)
    c_a = [ahead(a.at[j], a.at[j + 1], 2 + j) for j in range(3)]
    c_b = behind(b0, b_in, 5)
    c_e = behind(e1, e_in, 6)
    c_s1 = [ahead(s1.at[f], s1_in.at[f], 7 + f) for f in range(nfreq)]
    c_g1 = [
        ahead(g.at[f, pl.ds(4 * count, 2 * count)], g1_in.at[f], 7 + nfreq + f)
        for f in range(nfreq)
    ]
    c_g2 = [
        ahead(g.at[f, pl.ds(2 * count, 2 * count)], g2_in.at[f], 7 + 2 * nfreq + f)
        for f in range(nfreq)
    ]
    ups = [c_kup, *c_a, *c_s1, *c_g1, *c_g2]
    downs = [c_kdn, c_b, c_e]

    def start_up(c):
        pl.when(has_above)(c.start)

    def start_down(c):
        pl.when(has_below)(c.start)

    def take(c, there, ref, i=None):
        pl.when(there)(c.wait_recv)

        @pl.when(jnp.logical_not(there))
        def _():
            if i is None:
                ref[...] = jnp.zeros(ref.shape, ref.dtype)
            else:
                ref[i] = jnp.zeros(ref.shape[1:], ref.dtype)

    table[...] = angle_table(count, points)
    coef_in.wait()
    k0[...] = (cf[...] * table[...].astype(F32)).astype(BF)

    inside = jnp.logical_and(has_above, has_below)
    pl.when(inside)(lambda: pl.semaphore_wait(barrier, nf + 1))
    pl.when(jnp.logical_not(inside))(lambda: pl.semaphore_wait(barrier, nf))
    start_up(c_kup)
    start_down(c_kdn)

    def tiles(step):
        def one(c, carry):
            step(pl.ds(pl.multiple_of(c * TILE, TILE), TILE))
            return carry

        lax.fori_loop(0, points // TILE, one, 0)

    def real_times(rows, f, out, base):
        def step(cols):
            for p in range(2):
                out[f, pl.ds(base + p * count, count), cols] = dot(
                    rows[...], w[f, p, :, cols]
                ).astype(BF)

        tiles(step)

    def complex_times(rows, f, out, base):
        def step(cols):
            x = rows[f]
            first = dot(x, w[f, 0, :, cols])
            second = dot(x, w[f, 1, :, cols])
            out[f, pl.ds(base, count), cols] = (first[:count] - second[count:]).astype(BF)
            out[f, pl.ds(base + count, count), cols] = (first[count:] + second[:count]).astype(BF)

        tiles(step)

    src_in.wait()
    for f in range(nfreq):
        a[0, f] = dot(table[...], src[f]).astype(BF)
    start_up(c_a[0])

    for f in range(nfreq):
        w_in[f][0].wait()
        w_in[f][1].wait()
        real_times(table, f, s1, 0)
        start_up(c_s1[f])
        if f == 0:
            take(c_a[0], has_below, a, 1)
            start_up(c_a[1])
    take(c_kup, has_below, k_up)

    for f in range(nfreq):
        real_times(k_up, f, g, 4 * count)
        start_up(c_g1[f])
        if f == 0:
            take(c_a[1], has_below, a, 2)
            start_up(c_a[2])

    def mixed(pair, field):
        n = pair.shape[1] // 2
        return dot(pair[:, :n], field) + dot(pair[:, n:], turned(field))

    tg1 = []
    for f in range(nfreq):
        tg1.append(dot_nt(table[...], g[f, pl.ds(4 * count, 2 * count)]).astype(BF))
        b0[f] = mixed(tg1[f], a[1, f]).astype(BF)
    start_down(c_b)

    th1 = []
    for f in range(nfreq):
        take(c_s1[f], has_below, s1_in, f)
        complex_times(s1_in, f, s2, 0)
        th1.append(
            [dot_nt(s1_in[f, pl.ds(p * count, count)], k0[...]).astype(BF) for p in range(2)]
        )
        low = dot(th1[f][0], b0[f]) + dot(th1[f][1], turned(b0[f]))
        d1 = (a[1, f].astype(F32) - low).astype(BF)
        q[f, pl.ds(4 * count, count)] = d1
        q[f, pl.ds(5 * count, count)] = turned(d1)

    for f in range(nfreq):
        take(c_g1[f], has_below, g1_in, f)
        complex_times(g1_in, f, g, 2 * count)
        start_up(c_g2[f])

    take(c_kdn, has_above, k_dn)
    take(c_b, has_above, b_in)
    for f in range(nfreq):
        tg2 = dot_nt(table[...], g[f, pl.ds(2 * count, 2 * count)]).astype(BF)
        c0 = (mixed(tg2, a[2, f]) + mixed(tg1[f], a[1, f])).astype(BF)
        th2 = [dot_nt(s2[f, pl.ds(p * count, count)], k_dn[...]).astype(BF) for p in range(2)]
        e1[f] = (
            dot(th2[0], b_in[f])
            + dot(th2[1], turned(b_in[f]))
            + dot(th1[f][0], c0)
            + dot(th1[f][1], turned(c0))
        ).astype(BF)
    start_down(c_e)
    take(c_a[2], has_below, a, 3)
    for f in range(nfreq):
        q[f, pl.ds(0, count)] = a[3, f]
        q[f, pl.ds(count, count)] = turned(a[3, f])
        q[f, pl.ds(2 * count, count)] = a[2, f]
        q[f, pl.ds(3 * count, count)] = turned(a[2, f])
    take(c_e, has_above, e_in)
    for f in range(nfreq):
        fin[f] = (a[0, f].astype(F32) - e_in[f].astype(F32)).astype(BF)
    fin_copy = pltpu.make_async_copy(fin, fin_out, out_sem.at[nfreq + 2])
    fin_copy.start()

    up_copies = []
    for f in range(nfreq):
        take(c_g2[f], has_below, g2_in, f)
        complex_times(g2_in, f, g, 0)

        def field(cols):
            value = dot_tn(g[f, :, cols], q[f]).astype(BF)
            up_v[f, cols] = value
            corr = dot_nt(fin[f], value)
            if f == 0:
                grad_t[:, cols] = corr
            else:
                grad_t[:, cols] += corr

        tiles(field)
        up_copies.append(pltpu.make_async_copy(up_v.at[f], up_out.at[0, f], out_sem.at[f]))
        up_copies[f].start()

    scale = 1.0 / (half * nfreq * nf) ** 0.5
    grad_t[...] = grad_t[...] * scale
    part_s[...] = grad_t[...].astype(BF)
    c_f = [
        pltpu.make_async_remote_copy(
            part_s, part_in.at[d - 1], fsend.at[d - 1], frecv.at[d - 1],
            device_id={"freq": lax.rem(fme + d, nf)},
        )
        for d in range(1, nf)
    ]
    for c in c_f:
        c.start()
    for d, c in enumerate(c_f):
        c.wait_recv()
        grad_t[...] += part_in[d].astype(F32)

    rows = points // nf
    mine = pl.ds(pl.multiple_of(fme * rows, rows), rows)
    for c in c_f:
        c.wait_send()
    part_s[...] = ((cf[...] - grad_t[...]) * table[...].astype(F32)).astype(BF)
    last = [
        pltpu.make_async_copy(part_s, kernel_out, out_sem.at[nfreq]),
        pltpu.make_async_copy(grad_t.at[:, mine], grad_out.at[0], out_sem.at[nfreq + 1]),
        fin_copy,
    ]
    last[0].start()
    last[1].start()

    for c in ups:
        pl.when(has_above)(c.wait_send)
    for c in downs:
        pl.when(has_below)(c.wait_send)
    for c in (*up_copies, *last):
        c.wait()


def shine(up, grad, kernel, fin, up_out, grad_out, refl_out, up_v, grad_v, kt, fv, refl_v, sem, osem):
    nfreq, points, _ = up_v.shape
    first = [
        pltpu.make_async_copy(kernel, kt, sem.at[0]),
        pltpu.make_async_copy(fin, fv, sem.at[1]),
        pltpu.make_async_copy(up.at[0], up_v, sem.at[2]),
        pltpu.make_async_copy(grad, grad_v, sem.at[3]),
    ]
    for c in first:
        c.start()
    first[0].wait()
    first[1].wait()
    last = []
    for f in range(nfreq):
        refl_v[f] = dot_tn(kt[...], fv[f]).astype(BF)
        last.append(pltpu.make_async_copy(refl_v.at[f], refl_out.at[0, f], osem.at[f]))
        last[f].start()
    first[2].wait()
    last.append(pltpu.make_async_copy(up_v, up_out.at[0], osem.at[nfreq]))
    last[-1].start()
    first[3].wait()
    last.append(pltpu.make_async_copy(grad_v, grad_out, osem.at[nfreq + 1]))
    last[-1].start()
    for c in last:
        c.wait()


def solution(mesh):
    nd, nf = mesh.shape["depth"], mesh.shape["freq"]

    def local(propagator, incident, coeffs):
        _, nfreq, points, width = incident.shape
        count = coeffs.shape[2]
        rows = points // nf
        field = (nfreq, points, width)
        angles = (nfreq, count, width)
        messages = 7 + 3 * nfreq
        hbm = pl.BlockSpec(memory_space=pl.ANY)
        v = pltpu.VMEM
        up, grad, kernel, fin = pl.pallas_call(
            functools.partial(body, nd, nf),
            out_shape=(
                jax.ShapeDtypeStruct((1, *field), BF),
                jax.ShapeDtypeStruct((1, count, rows), F32),
                jax.ShapeDtypeStruct((count, points), BF),
                jax.ShapeDtypeStruct(angles, BF),
            ),
            in_specs=[hbm] * 3,
            out_specs=[hbm] * 4,
            scratch_shapes=[
                v((nfreq, 2, points, points), BF),
                v(field, BF),
                v((count, points), F32),
                v((count, points), BF),
                v((count, points), BF),
                v((count, points), BF),
                v((count, points), BF),
                v((4, *angles), BF),
                v((nfreq, 6 * count, width), BF),
                v((nfreq, 2 * count, points), BF),
                v((nfreq, 2 * count, points), BF),
                v((nfreq, 2 * count, points), BF),
                v((nfreq, 6 * count, points), BF),
                v((nfreq, 2 * count, points), BF),
                v((nfreq, 2 * count, points), BF),
                v(angles, BF),
                v(angles, BF),
                v(angles, BF),
                v(angles, BF),
                v(angles, BF),
                v(field, BF),
                v((count, points), BF),
                v((max(nf - 1, 1), count, points), BF),
                v((count, points), F32),
                pltpu.SemaphoreType.DMA((2 + 2 * nfreq,)),
                pltpu.SemaphoreType.DMA((nfreq + 3,)),
                pltpu.SemaphoreType.DMA((messages,)),
                pltpu.SemaphoreType.DMA((messages,)),
                pltpu.SemaphoreType.DMA((max(nf - 1, 1),)),
                pltpu.SemaphoreType.DMA((max(nf - 1, 1),)),
            ],
            compiler_params=pltpu.CompilerParams(
                collective_id=0, has_side_effects=True, vmem_limit_bytes=60 * 1024 * 1024
            ),
            name="bremmer",
        )(propagator, incident, jnp.swapaxes(coeffs, 1, 2))
        up, grad, reflected = pl.pallas_call(
            shine,
            out_shape=(
                jax.ShapeDtypeStruct((1, *field), BF),
                jax.ShapeDtypeStruct((1, count, rows), F32),
                jax.ShapeDtypeStruct((1, *field), BF),
            ),
            in_specs=[hbm] * 4,
            out_specs=[hbm] * 3,
            scratch_shapes=[
                v(field, BF),
                v((1, count, rows), F32),
                v((count, points), BF),
                v(angles, BF),
                v(field, BF),
                pltpu.SemaphoreType.DMA((4,)),
                pltpu.SemaphoreType.DMA((nfreq + 2,)),
            ],
            compiler_params=pltpu.CompilerParams(vmem_limit_bytes=60 * 1024 * 1024),
            name="shine",
        )(up, grad, kernel, fin)
        return up, jnp.swapaxes(grad, 1, 2), reflected

    return jax.shard_map(
        local,
        mesh=mesh,
        in_specs=(
            P("depth", "freq", None, None, None),
            P("depth", "freq", None, None),
            P("depth", None, None),
        ),
        out_specs=(
            P("depth", "freq", None, None),
            P("depth", "freq", None),
            P("depth", "freq", None, None),
        ),
        check_vma=False,
    )
```

```python
import functools

import jax
import jax.numpy as jnp
from jax import lax
from jax.experimental import pallas as pl
from jax.experimental.pallas import tpu as pltpu
from jax.sharding import PartitionSpec as P

BF = jnp.bfloat16
F32 = jnp.float32
TILE = 512


def dot(a, b):
    return jnp.dot(a, b, preferred_element_type=F32)


def dot_nt(a, b):
    return lax.dot_general(a, b, (((1,), (1,)), ((), ())), preferred_element_type=F32)


def dot_tn(a, b):
    return lax.dot_general(a, b, (((0,), (0,)), ((), ())), preferred_element_type=F32)


def turned(field):
    half = field.shape[-1] // 2
    return jnp.concatenate([-field[:, half:], field[:, :half]], 1)


def angle_table(count, points):
    angle = lax.broadcasted_iota(jnp.int32, (count, points), 0).astype(F32) + 0.5
    place = lax.broadcasted_iota(jnp.int32, (count, points), 1).astype(F32) + 0.5
    return ((2.0 / points) ** 0.5 * jnp.cos(jnp.pi * angle * place / points)).astype(BF)


def body(
    nd, nf, prop, inc, coef, up_out, grad_out, kernel_out, fin_out,
    w, src, cf, table, k0, k_up, k_dn, a, q, s1, s1_in, s2, g, g1_in, g2_in,
    b0, b_in, e1, e_in, fin, up_v, part_s, part_in, grad_t,
    in_sem, out_sem, send, recv, fsend, frecv,
):
    me = lax.axis_index("depth")
    fme = lax.axis_index("freq")
    nfreq, _, points, _ = w.shape
    count = table.shape[0]
    half = src.shape[2] // 2
    has_above = me > 0
    has_below = me < nd - 1
    above = lax.rem(me + nd - 1, nd)
    below = lax.rem(me + 1, nd)

    coef_in = pltpu.make_async_copy(coef.at[0], cf, in_sem.at[0])
    src_in = pltpu.make_async_copy(inc.at[0], src, in_sem.at[1])
    w_in = [
        [
            pltpu.make_async_copy(prop.at[0, f, p], w.at[f, p], in_sem.at[2 + 2 * f + p])
            for p in range(2)
        ]
        for f in range(nfreq)
    ]
    coef_in.start()
    src_in.start()
    for f in range(nfreq):
        w_in[f][0].start()
        w_in[f][1].start()

    barrier = pltpu.get_barrier_semaphore()

    @pl.when(has_above)
    def _():
        pl.semaphore_signal(barrier, 1, device_id={"depth": above})

    @pl.when(has_below)
    def _():
        pl.semaphore_signal(barrier, 1, device_id={"depth": below})

    for d in range(1, nf):
        pl.semaphore_signal(barrier, 1, device_id={"freq": lax.rem(fme + d, nf)})

    def ahead(x, y, i):
        return pltpu.make_async_remote_copy(
            x, y, send.at[i], recv.at[i], device_id={"depth": above}
        )

    def behind(x, y, i):
        return pltpu.make_async_remote_copy(
            x, y, send.at[i], recv.at[i], device_id={"depth": below}
        )

    c_kup = ahead(k0, k_up, 0)
    c_kdn = behind(k0, k_dn, 1)
    c_a = [ahead(a.at[j], a.at[j + 1], 2 + j) for j in range(3)]
    c_b = behind(b0, b_in, 5)
    c_e = behind(e1, e_in, 6)
    c_s1 = [ahead(s1.at[f], s1_in.at[f], 7 + f) for f in range(nfreq)]
    c_g1 = [
        ahead(g.at[f, pl.ds(4 * count, 2 * count)], g1_in.at[f], 7 + nfreq + f)
        for f in range(nfreq)
    ]
    c_g2 = [
        ahead(g.at[f, pl.ds(2 * count, 2 * count)], g2_in.at[f], 7 + 2 * nfreq + f)
        for f in range(nfreq)
    ]
    ups = [c_kup, *c_a, *c_s1, *c_g1, *c_g2]
    downs = [c_kdn, c_b, c_e]

    def start_up(c):
        pl.when(has_above)(c.start)

    def start_down(c):
        pl.when(has_below)(c.start)

    def take(c, there, ref, i=None):
        pl.when(there)(c.wait_recv)

        @pl.when(jnp.logical_not(there))
        def _():
            if i is None:
                ref[...] = jnp.zeros(ref.shape, ref.dtype)
            else:
                ref[i] = jnp.zeros(ref.shape[1:], ref.dtype)

    table[...] = angle_table(count, points)
    coef_in.wait()
    k0[...] = (cf[...] * table[...].astype(F32)).astype(BF)

    inside = jnp.logical_and(has_above, has_below)
    pl.when(inside)(lambda: pl.semaphore_wait(barrier, nf + 1))
    pl.when(jnp.logical_not(inside))(lambda: pl.semaphore_wait(barrier, nf))
    start_up(c_kup)
    start_down(c_kdn)

    def tiles(step):
        def one(c, carry):
            step(pl.ds(pl.multiple_of(c * TILE, TILE), TILE))
            return carry

        lax.fori_loop(0, points // TILE, one, 0, unroll=True)

    def real_times(rows, f, out, base):
        def step(cols):
            for p in range(2):
                out[f, pl.ds(base + p * count, count), cols] = dot(
                    rows[...], w[f, p, :, cols]
                ).astype(BF)

        tiles(step)

    def second_times(f):
        def step(cols):
            x = jnp.concatenate([s1_in[f], g1_in[f]], 0)
            y = dot(x, w[f, 0, :, cols])
            z = dot(x, w[f, 1, :, cols])
            n = count
            s2[f, pl.ds(0, n), cols] = (y[:n] - z[n : 2 * n]).astype(BF)
            s2[f, pl.ds(n, n), cols] = (y[n : 2 * n] + z[:n]).astype(BF)
            g[f, pl.ds(2 * n, n), cols] = (y[2 * n : 3 * n] - z[3 * n :]).astype(BF)
            g[f, pl.ds(3 * n, n), cols] = (y[3 * n :] + z[2 * n : 3 * n]).astype(BF)

        tiles(step)

    def complex_times(rows, f, out, base):
        def step(cols):
            x = rows[f]
            first = dot(x, w[f, 0, :, cols])
            second = dot(x, w[f, 1, :, cols])
            out[f, pl.ds(base, count), cols] = (first[:count] - second[count:]).astype(BF)
            out[f, pl.ds(base + count, count), cols] = (first[count:] + second[:count]).astype(BF)

        tiles(step)

    src_in.wait()
    for f in range(nfreq):
        a[0, f] = dot(table[...], src[f]).astype(BF)
    start_up(c_a[0])

    for f in range(nfreq):
        w_in[f][0].wait()
        w_in[f][1].wait()
        real_times(table, f, s1, 0)
        start_up(c_s1[f])
        if f == 0:
            take(c_a[0], has_below, a, 1)
            start_up(c_a[1])
    take(c_kup, has_below, k_up)

    for f in range(nfreq):
        real_times(k_up, f, g, 4 * count)
        start_up(c_g1[f])
        if f == 0:
            take(c_a[1], has_below, a, 2)
            start_up(c_a[2])

    def mixed(pair, field):
        n = pair.shape[1] // 2
        return dot(pair[:, :n], field) + dot(pair[:, n:], turned(field))

    tg1 = []
    for f in range(nfreq):
        tg1.append(dot_nt(table[...], g[f, pl.ds(4 * count, 2 * count)]).astype(BF))
        b0[f] = mixed(tg1[f], a[1, f]).astype(BF)
    start_down(c_b)

    th1 = []
    for f in range(nfreq):
        take(c_s1[f], has_below, s1_in, f)
        take(c_g1[f], has_below, g1_in, f)
        second_times(f)
        start_up(c_g2[f])
        th1.append(
            [dot_nt(s1_in[f, pl.ds(p * count, count)], k0[...]).astype(BF) for p in range(2)]
        )
        low = dot(th1[f][0], b0[f]) + dot(th1[f][1], turned(b0[f]))
        d1 = (a[1, f].astype(F32) - low).astype(BF)
        q[f, pl.ds(4 * count, count)] = d1
        q[f, pl.ds(5 * count, count)] = turned(d1)

    take(c_kdn, has_above, k_dn)
    take(c_b, has_above, b_in)
    for f in range(nfreq):
        tg2 = dot_nt(table[...], g[f, pl.ds(2 * count, 2 * count)]).astype(BF)
        c0 = (mixed(tg2, a[2, f]) + mixed(tg1[f], a[1, f])).astype(BF)
        th2 = [dot_nt(s2[f, pl.ds(p * count, count)], k_dn[...]).astype(BF) for p in range(2)]
        e1[f] = (
            dot(th2[0], b_in[f])
            + dot(th2[1], turned(b_in[f]))
            + dot(th1[f][0], c0)
            + dot(th1[f][1], turned(c0))
        ).astype(BF)
    start_down(c_e)
    take(c_a[2], has_below, a, 3)
    for f in range(nfreq):
        q[f, pl.ds(0, count)] = a[3, f]
        q[f, pl.ds(count, count)] = turned(a[3, f])
        q[f, pl.ds(2 * count, count)] = a[2, f]
        q[f, pl.ds(3 * count, count)] = turned(a[2, f])
    take(c_e, has_above, e_in)
    for f in range(nfreq):
        fin[f] = (a[0, f].astype(F32) - e_in[f].astype(F32)).astype(BF)
    fin_copy = pltpu.make_async_copy(fin, fin_out, out_sem.at[nfreq + 2])
    fin_copy.start()

    up_copies = []
    for f in range(nfreq):
        take(c_g2[f], has_below, g2_in, f)
        complex_times(g2_in, f, g, 0)

        def field(cols):
            value = dot_tn(g[f, :, cols], q[f]).astype(BF)
            up_v[f, cols] = value
            corr = dot_nt(fin[f], value)
            if f == 0:
                grad_t[:, cols] = corr
            else:
                grad_t[:, cols] += corr

        tiles(field)
        up_copies.append(pltpu.make_async_copy(up_v.at[f], up_out.at[0, f], out_sem.at[f]))
        up_copies[f].start()

    scale = 1.0 / (half * nfreq * nf) ** 0.5
    grad_t[...] = grad_t[...] * scale
    part_s[...] = grad_t[...].astype(BF)
    c_f = [
        pltpu.make_async_remote_copy(
            part_s, part_in.at[d - 1], fsend.at[d - 1], frecv.at[d - 1],
            device_id={"freq": lax.rem(fme + d, nf)},
        )
        for d in range(1, nf)
    ]
    for c in c_f:
        c.start()
    for d, c in enumerate(c_f):
        c.wait_recv()
        grad_t[...] += part_in[d].astype(F32)

    rows = points // nf
    mine = pl.ds(pl.multiple_of(fme * rows, rows), rows)
    for c in c_f:
        c.wait_send()
    part_s[...] = ((cf[...] - grad_t[...]) * table[...].astype(F32)).astype(BF)
    last = [
        pltpu.make_async_copy(part_s, kernel_out, out_sem.at[nfreq]),
        pltpu.make_async_copy(grad_t.at[:, mine], grad_out.at[0], out_sem.at[nfreq + 1]),
        fin_copy,
    ]
    last[0].start()
    last[1].start()

    for c in ups:
        pl.when(has_above)(c.wait_send)
    for c in downs:
        pl.when(has_below)(c.wait_send)
    for c in (*up_copies, *last):
        c.wait()


def shine(up, grad, kernel, fin, up_out, grad_out, refl_out, up_v, grad_v, kt, fv, refl_v, sem, osem):
    nfreq, points, _ = up_v.shape
    first = [
        pltpu.make_async_copy(kernel, kt, sem.at[0]),
        pltpu.make_async_copy(fin, fv, sem.at[1]),
        pltpu.make_async_copy(up.at[0], up_v, sem.at[2]),
        pltpu.make_async_copy(grad, grad_v, sem.at[3]),
    ]
    for c in first:
        c.start()
    first[0].wait()
    first[1].wait()
    last = []
    for f in range(nfreq):
        refl_v[f] = dot_tn(kt[...], fv[f]).astype(BF)
        last.append(pltpu.make_async_copy(refl_v.at[f], refl_out.at[0, f], osem.at[f]))
        last[f].start()
    first[2].wait()
    last.append(pltpu.make_async_copy(up_v, up_out.at[0], osem.at[nfreq]))
    last[-1].start()
    first[3].wait()
    last.append(pltpu.make_async_copy(grad_v, grad_out, osem.at[nfreq + 1]))
    last[-1].start()
    for c in last:
        c.wait()


def solution(mesh):
    nd, nf = mesh.shape["depth"], mesh.shape["freq"]

    def local(propagator, incident, coeffs):
        _, nfreq, points, width = incident.shape
        count = coeffs.shape[2]
        rows = points // nf
        field = (nfreq, points, width)
        angles = (nfreq, count, width)
        messages = 7 + 3 * nfreq
        hbm = pl.BlockSpec(memory_space=pl.ANY)
        v = pltpu.VMEM
        up, grad, kernel, fin = pl.pallas_call(
            functools.partial(body, nd, nf),
            out_shape=(
                jax.ShapeDtypeStruct((1, *field), BF),
                jax.ShapeDtypeStruct((1, count, rows), F32),
                jax.ShapeDtypeStruct((count, points), BF),
                jax.ShapeDtypeStruct(angles, BF),
            ),
            in_specs=[hbm] * 3,
            out_specs=[hbm] * 4,
            scratch_shapes=[
                v((nfreq, 2, points, points), BF),
                v(field, BF),
                v((count, points), F32),
                v((count, points), BF),
                v((count, points), BF),
                v((count, points), BF),
                v((count, points), BF),
                v((4, *angles), BF),
                v((nfreq, 6 * count, width), BF),
                v((nfreq, 2 * count, points), BF),
                v((nfreq, 2 * count, points), BF),
                v((nfreq, 2 * count, points), BF),
                v((nfreq, 6 * count, points), BF),
                v((nfreq, 2 * count, points), BF),
                v((nfreq, 2 * count, points), BF),
                v(angles, BF),
                v(angles, BF),
                v(angles, BF),
                v(angles, BF),
                v(angles, BF),
                v(field, BF),
                v((count, points), BF),
                v((max(nf - 1, 1), count, points), BF),
                v((count, points), F32),
                pltpu.SemaphoreType.DMA((2 + 2 * nfreq,)),
                pltpu.SemaphoreType.DMA((nfreq + 3,)),
                pltpu.SemaphoreType.DMA((messages,)),
                pltpu.SemaphoreType.DMA((messages,)),
                pltpu.SemaphoreType.DMA((max(nf - 1, 1),)),
                pltpu.SemaphoreType.DMA((max(nf - 1, 1),)),
            ],
            compiler_params=pltpu.CompilerParams(
                collective_id=0, has_side_effects=True, vmem_limit_bytes=60 * 1024 * 1024
            ),
            name="bremmer",
        )(propagator, incident, jnp.swapaxes(coeffs, 1, 2))
        up, grad, reflected = pl.pallas_call(
            shine,
            out_shape=(
                jax.ShapeDtypeStruct((1, *field), BF),
                jax.ShapeDtypeStruct((1, count, rows), F32),
                jax.ShapeDtypeStruct((1, *field), BF),
            ),
            in_specs=[hbm] * 4,
            out_specs=[hbm] * 3,
            scratch_shapes=[
                v(field, BF),
                v((1, count, rows), F32),
                v((count, points), BF),
                v(angles, BF),
                v(field, BF),
                pltpu.SemaphoreType.DMA((4,)),
                pltpu.SemaphoreType.DMA((nfreq + 2,)),
            ],
            compiler_params=pltpu.CompilerParams(vmem_limit_bytes=60 * 1024 * 1024),
            name="shine",
        )(up, grad, kernel, fin)
        return up, jnp.swapaxes(grad, 1, 2), reflected

    return jax.shard_map(
        local,
        mesh=mesh,
        in_specs=(
            P("depth", "freq", None, None, None),
            P("depth", "freq", None, None),
            P("depth", None, None),
        ),
        out_specs=(
            P("depth", "freq", None, None),
            P("depth", "freq", None),
            P("depth", "freq", None, None),
        ),
        check_vma=False,
    )
```
